32 devices in a mesh: grp: 2 (over y), gx: 4 (over z), row: 2 (over x), pb: 2 (over core).
Axes of the slice: x: 2, y: 2, z: 4, core: 2. Of those that a mesh axis runs over, the one named last changes fastest.
Arguments:
- features: bfloat16 [2048, 16, 512], P(('grp', 'gx', 'row')), parts along dimension 0, may hold values from -720 to 720
- query_pool: bfloat16 [512, 16, 512], P(None, 'gx'), may hold values from -6 to 6
- query_ids: int32 [256], P('pb'), may hold values from 0 to 511
Outputs:
- scores: float32 [2048, 256], P(('grp', 'gx', 'row'), 'pb'), parts along dimension 0
The draws below stay inside these ranges and needn't reach their ends.
There are 2 independent parts, one for each index of `grp`. The reference program is written for one: setup_inputs(seed, part) draws one part's arguments, and reference() takes and returns one part's arrays. A program takes and returns all parts, laid end to end along the dimension named above; an argument that names none is the same for every part. Nothing has to cross between parts.
All inputs are finite; a program needn't handle non-finite values.
Results may differ from the reference program's by a relative error of at most 0.0035.
Values may be sent and summed in bfloat16 or wider, within the bound.
No kernel may reach another device: no remote copies, remote signals or barrier semaphores. Data moves between devices by JAX's collectives and lax.ppermute only.
A program may use at most 64 MiB of HBM per device.

```python
import math
import jax
import jax.numpy as jnp
from jax import lax

FEAT = 512
MODULES = 16
QUERIES = 256
POOL = 512
ITERS = 4
EXAMPLES = 1024


def draw_features(key, part):
    key_base, key_cols, key_rows = jax.random.split(key, 3)
    shape = (EXAMPLES, MODULES, FEAT)
    base = jax.random.normal(key_base, shape, jnp.float32)
    base = jnp.clip(base, -4.0, 4.0)
    cols = jnp.exp(jax.random.uniform(key_cols, (1, MODULES, FEAT), jnp.float32) * math.log(10.0))
    rows = jnp.exp(jax.random.uniform(key_rows, (EXAMPLES, 1, 1), jnp.float32) * math.log(2.0))
    rise = 1.0 + 2.0 * jnp.arange(EXAMPLES, dtype=jnp.float32) / EXAMPLES
    modrise = 1.0 + 2.0 * jnp.arange(MODULES, dtype=jnp.float32) / MODULES
    values = base * cols * rows * rise[:, None, None] * modrise[None, :, None]
    return values.astype(jnp.bfloat16)


def plant(values, rng, low, top_value):
    longest = values.shape.index(max(values.shape))
    spots = []
    for shift in (0, 1):
        where = [jax.random.randint(jax.random.fold_in(rng, axis), (), 0, length) for axis, length in enumerate(values.shape)]
        where[longest] = (where[longest] + shift) % values.shape[longest]
        spots.append(tuple(where))
    return values.at[spots[0]].set(low).at[spots[1]].set(top_value)


def shard_levels(key, extent, shards, low, largest):
    gain, own = 1.0, jax.random.fold_in(key, 6)
    for dim, parts in shards:
        heights = jnp.exp(jax.random.uniform(jax.random.fold_in(own, dim), (parts,), jnp.float32, low / len(shards), largest / len(shards)))
        gain = gain * jnp.repeat(heights, extent[dim] // parts).reshape([-1 if axis == dim else 1 for axis in range(len(extent))])
    return gain


def noise(stream_key, shape, spread, limit, shards=(), kind=jnp.bfloat16):
    loudness = shard_levels(stream_key, shape, shards, -0.22, 0.18) if shards else 1.0
    entries = jax.random.normal(stream_key, shape, jnp.float32) * spread * loudness
    return jnp.minimum(jnp.maximum(entries, -limit), limit).astype(kind)


def setup_inputs(seed: int = 0, part: int = 0) -> dict:
    key_list = jax.random.split(jax.random.key(seed), 4)
    own_keys = jax.random.split(jax.random.fold_in(key_list[3], part), 4)
    return {
        "features": draw_features(jax.random.fold_in(jax.random.fold_in(key_list[3], part), 71), part),
        "query_pool": noise(key_list[1], (POOL, MODULES, FEAT), 1.0, 6.0, ((1, 4),)),
        "query_ids": plant(jax.random.randint(key_list[2], (QUERIES,), 0, POOL), jax.random.fold_in(key_list[2], 1), 0, POOL - 1).astype(jnp.int32),
    }


def reference(features, query_pool, query_ids):
    count = features.shape[0]
    modules = features.shape[1]
    feat = features.shape[2]
    by_module = jnp.transpose(features, (1, 0, 2))
    grams = lax.map(lambda block: jnp.dot(block.T, block, preferred_element_type=jnp.float32), by_module)
    total = jnp.sum(jnp.trace(grams, axis1=1, axis2=2))
    damping = 0.5 * total / (count * modules * feat)
    identity = jnp.eye(feat, dtype=jnp.float32)
    hessian = grams / count + damping * identity
    frob = jnp.sqrt(lax.optimization_barrier(jnp.sum(hessian * hessian, axis=(1, 2))) + 1e-06)
    inverse = identity[None] / frob[:, None, None]
    for step in range(ITERS):
        product = jnp.matmul(hessian, inverse, precision=lax.Precision.HIGHEST)
        inverse = 2.0 * inverse - jnp.matmul(inverse, product, precision=lax.Precision.HIGHEST)
    picked = query_pool[query_ids.astype(jnp.int32)]
    precond = jnp.einsum('qmk,mkj->qmj', picked.astype(jnp.float32), inverse, precision=lax.Precision.HIGHEST).astype(jnp.bfloat16)
    flat_rows = features.reshape(count, modules * feat)
    flat_query = precond.reshape(precond.shape[0], modules * feat)
    return jnp.dot(flat_rows, flat_query.T, preferred_element_type=jnp.float32)
```

```python
import functools

import jax
import jax.numpy as jnp
from jax import lax
from jax.experimental import pallas as pl
from jax.experimental.pallas import tpu as pltpu
from jax.sharding import PartitionSpec as P

ITERS = 4
BF16 = jnp.bfloat16
F32 = jnp.float32
LANES = 128
GROUP = ("gx", "row")
VMEM = pl.BlockSpec(memory_space=pltpu.VMEM)


def dot(a, b, dims):
    return lax.dot_general(a, b, (dims, ((), ())), preferred_element_type=F32)


def split(a):
    high = a.astype(BF16)
    return high, (a - high.astype(F32)).astype(BF16)


def pack_kernel(peers, feats, *outs):
    ex_dev, modules, feat = feats.shape
    cols = feat // LANES
    step = 256 // modules
    me = lax.axis_index("gx") * lax.axis_size("row") + lax.axis_index("row")
    side = lax.axis_index("pb")
    r = lax.broadcasted_iota(jnp.int32, (peers * step, step * modules), 0)
    c = lax.broadcasted_iota(jnp.int32, (peers * step, step * modules), 1)
    wanted = ((r // step) ^ me) * lax.axis_size("pb") + side
    pick = ((c // modules == r % step) & (c % modules == wanted)).astype(F32).astype(BF16)

    def body(b, acc):
        x = feats[pl.ds(b * step, step)].reshape(step * modules, feat)
        y = dot(pick, x, ((1,), (0,))).astype(BF16)
        for k in range(peers):
            for j in range(cols):
                start = pl.multiple_of(j * ex_dev + b * step, step)
                outs[k][pl.ds(start, step), :] = y[k * step : (k + 1) * step, j * LANES : (j + 1) * LANES]
        xf = x.astype(F32)
        sq = xf * xf
        return acc + sq.reshape(step * modules // 8, 8, feat).sum(0)

    acc = lax.fori_loop(0, ex_dev // step, body, jnp.zeros((8, feat), F32))
    lane = acc.sum(0, keepdims=True)
    lane = sum(lane[:, j * LANES : (j + 1) * LANES] for j in range(cols))
    high, rest = split(lane)
    mid, low = split(lane - high.astype(F32))
    row = lax.broadcasted_iota(jnp.int32, (8, LANES), 0)
    high, mid, low = (jnp.broadcast_to(v.astype(F32), (8, LANES)) for v in (high, mid, low))
    tail = jnp.where(row == 0, high, jnp.where(row == 1, mid, jnp.where(row == 2, low, 0.0)))
    for k in range(peers):
        outs[k][pl.ds(cols * ex_dev, 8), :] = tail.astype(BF16)


def pack(features, peers):
    ex_dev, modules, feat = features.shape
    shape = jax.ShapeDtypeStruct((feat // LANES * ex_dev + 8, LANES), BF16)
    return pl.pallas_call(
        functools.partial(pack_kernel, peers),
        out_shape=[shape] * peers,
        in_specs=[VMEM],
        out_specs=[VMEM] * peers,
        name="pack",
    )(features)


def pick_kernel(pool, ids, out):
    rows, queries = pool.shape[0] * pool.shape[1], ids.shape[1]
    local = lax.axis_index("row") * lax.axis_size("pb") + lax.axis_index("pb")
    wanted = ids[...] * pool.shape[1] + local
    r = lax.broadcasted_iota(jnp.int32, (rows, queries), 0)
    chosen = (r == wanted).astype(F32).astype(BF16)
    flat = pool[...].reshape(rows, pool.shape[2])
    out[...] = dot(chosen, flat, ((0,), (0,))).astype(BF16)


def pick(query_pool, ids):
    return pl.pallas_call(
        pick_kernel,
        out_shape=jax.ShapeDtypeStruct((ids.shape[1], query_pool.shape[2]), BF16),
        in_specs=[VMEM, VMEM],
        out_specs=VMEM,
        name="pick",
    )(query_pool, ids)


def score_kernel(modules, *refs):
    peers = len(refs) - 4
    chunks, (picked, own, other, feats) = refs[:peers], refs[peers:]
    count, feat = feats.shape
    ex_dev = count // peers
    cols = feat // LANES
    total = jnp.zeros((1, LANES), F32)
    for k in range(peers):
        for j in range(cols):
            feats[k * ex_dev : (k + 1) * ex_dev, j * LANES : (j + 1) * LANES] = chunks[k][j * ex_dev : (j + 1) * ex_dev, :]
        total = total + chunks[k][cols * ex_dev :, :].astype(F32).sum(0, keepdims=True)
    total = jnp.sum(total)
    damping = 0.5 * total / (count * modules * feat)
    f = feats[...]
    gram = dot(f, f, ((0,), (0,)))
    diag = lax.broadcasted_iota(jnp.int32, (feat, feat), 0) == lax.broadcasted_iota(jnp.int32, (feat, feat), 1)
    hessian = gram / count + jnp.where(diag, damping, 0.0)
    inv = 1.0 / jnp.sqrt(jnp.sum(hessian * hessian) + 1e-06)
    plain = ((1,), (0,))

    def apply(v, mat):
        vh, vl = split(v)
        mh, ml = mat
        return dot(vh, mh, plain) + (dot(vl, mh, plain) + dot(vh, ml, plain))

    b1 = hessian * inv
    m1 = split(b1)
    b2 = 2.0 * b1 - dot(m1[0], m1[0], plain)
    m2 = split(b2)
    b4 = 2.0 * b2 - dot(m2[0], m2[0], plain)
    m4 = split(b4)
    v = picked[...]
    v = 2.0 * v.astype(F32) - (dot(v, m1[0], plain) + dot(v, m1[1], plain))
    v = 2.0 * v - apply(v, m2)
    v = 2.0 * v - apply(v, m4)
    w = v - apply(v, m4)
    w = w - apply(w, m4)
    precond = ((v + w) * inv).astype(BF16)
    half = precond.shape[0] // 2
    other[...] = dot(f, precond[half:], ((1,), (1,)))
    own[...] = dot(f, precond[:half], ((1,), (1,)))


def score(chunks, picked, modules):
    peers = len(chunks)
    queries, feat = picked.shape
    count = peers * (chunks[0].shape[0] - 8) * LANES // feat
    half = jax.ShapeDtypeStruct((count, queries // 2), F32)
    return pl.pallas_call(
        functools.partial(score_kernel, modules),
        out_shape=[half, half],
        in_specs=[VMEM] * (peers + 1),
        out_specs=[VMEM, VMEM],
        scratch_shapes=[pltpu.VMEM((count, feat), BF16)],
        name="score",
    )(*chunks, picked)


def exchange(x, axes, k, size):
    return lax.ppermute(x, axes, [(i, i ^ k) for i in range(size)])


def owned(features, query_pool, query_ids):
    ex_dev, modules, feat = features.shape
    peers = lax.axis_size("gx") * lax.axis_size("row")
    ids = jnp.concatenate([query_ids, exchange(query_ids, "pb", 1, 2)])[None, :]
    chunks = list(pack(features, peers))
    for k in (6, 7, 4, 5, 2, 3, 1):
        chunks[k] = exchange(chunks[k], GROUP, k, peers)
    picked = pick(query_pool, ids)
    own, other = score(chunks, picked, modules)
    part = own + exchange(other, "pb", 1, 2)
    part = part.reshape(2, 4, ex_dev, -1)
    near = part[:, 0]
    for k in (1, 2, 3):
        near = near + exchange(part[:, k].astype(BF16), GROUP, k, peers).astype(F32)
    return near[0] + exchange(near[1].astype(BF16), GROUP, 4, peers).astype(F32)


def regrouped(features, query_pool, query_ids):
    ex_dev, modules, feat = features.shape
    regrouped = lax.all_to_all(features, "gx", split_axis=1, concat_axis=0, tiled=True)
    count = regrouped.shape[0] * lax.axis_size("row")
    grams = jnp.einsum("emk,emj->mkj", regrouped, regrouped, preferred_element_type=jnp.float32)
    grams = lax.psum(grams, "row")
    total = lax.psum(jnp.sum(jnp.trace(grams, axis1=1, axis2=2)), "gx")
    damping = 0.5 * total / (count * modules * feat)
    identity = jnp.eye(feat, dtype=jnp.float32)
    hessian = grams / count + damping * identity
    frob = jnp.sqrt(jnp.sum(hessian * hessian, axis=(1, 2)) + 1e-06)
    inverse = identity[None] / frob[:, None, None]
    for step in range(ITERS):
        product = jnp.matmul(hessian, inverse, precision=lax.Precision.HIGHEST)
        inverse = 2.0 * inverse - jnp.matmul(inverse, product, precision=lax.Precision.HIGHEST)
    picked = jnp.take(query_pool, query_ids, axis=0)
    precond = jnp.einsum(
        "qmk,mkj->qmj", picked.astype(jnp.float32), inverse, precision=lax.Precision.HIGHEST
    ).astype(jnp.bfloat16)
    local_queries = precond.shape[0]
    flat_query = precond.reshape(local_queries, -1)
    return lax.psum_scatter(
        jnp.einsum(
            "ea,qa->eq",
            regrouped.reshape(ex_dev * lax.axis_size("gx"), -1),
            flat_query,
            preferred_element_type=jnp.float32,
        ),
        "gx",
        scatter_dimension=0,
        tiled=True,
    )


def shards(features, query_pool, query_ids):
    modules = features.shape[1]
    gx, row, pb = (lax.axis_size(name) for name in ("gx", "row", "pb"))
    if (gx, row, pb) == (4, 2, 2) and modules == gx * row * pb:
        return owned(features, query_pool, query_ids)
    return regrouped(features, query_pool, query_ids)


def solution(mesh):
    in_specs = (P(("grp", "gx", "row"), None, None), P(None, "gx", None), P("pb"))
    out_specs = P(("grp", "gx", "row"), "pb")
    return jax.shard_map(shards, mesh=mesh, in_specs=in_specs, out_specs=out_specs, check_vma=False)
```

```python
import functools

import jax
import jax.numpy as jnp
from jax import lax
from jax.experimental import pallas as pl
from jax.experimental.pallas import tpu as pltpu
from jax.sharding import PartitionSpec as P

ITERS = 4
BF16 = jnp.bfloat16
F32 = jnp.float32
LANES = 128
GROUP = ("gx", "row")
VMEM = pl.BlockSpec(memory_space=pltpu.VMEM)
ORDER = (7, 5, 6, 4, 3, 2, 1, 0)
NEAR = (1, 2, 3)
PLAIN = ((1,), (0,))


def limit(mib):
    return pltpu.CompilerParams(vmem_limit_bytes=mib << 20)


def dot(a, b, dims):
    return lax.dot_general(a, b, (dims, ((), ())), preferred_element_type=F32)


def split(a):
    high = a.astype(BF16)
    return high, (a - high.astype(F32)).astype(BF16)


def pack_kernel(peers, feats, *ordered):
    outs = dict(zip(ORDER, ordered))
    ex_dev, modules, feat = feats.shape
    cols = feat // LANES
    step = 256 // modules
    me = lax.axis_index("gx") * lax.axis_size("row") + lax.axis_index("row")
    side = lax.axis_index("pb")
    r = lax.broadcasted_iota(jnp.int32, (peers * step, step * modules), 0)
    c = lax.broadcasted_iota(jnp.int32, (peers * step, step * modules), 1)
    wanted = ((r // step) ^ me) * lax.axis_size("pb") + side
    pick = ((c // modules == r % step) & (c % modules == wanted)).astype(F32).astype(BF16)

    acc = jnp.zeros((8, feat), F32)
    for b in range(ex_dev // step):
        x = feats[b * step : (b + 1) * step].reshape(step * modules, feat)
        y = dot(pick, x, ((1,), (0,))).astype(BF16)
        for k in range(peers):
            for j in range(cols):
                start = j * ex_dev + b * step
                outs[k][start : start + step, :] = y[k * step : (k + 1) * step, j * LANES : (j + 1) * LANES]
        xf = x.astype(F32)
        sq = xf * xf
        acc = acc + sq.reshape(step * modules // 8, 8, feat).sum(0)
    lane = acc.sum(0, keepdims=True)
    lane = sum(lane[:, j * LANES : (j + 1) * LANES] for j in range(cols))
    high, rest = split(lane)
    mid, low = split(lane - high.astype(F32))
    row = lax.broadcasted_iota(jnp.int32, (8, LANES), 0)
    high, mid, low = (jnp.broadcast_to(v.astype(F32), (8, LANES)) for v in (high, mid, low))
    tail = jnp.where(row == 0, high, jnp.where(row == 1, mid, jnp.where(row == 2, low, 0.0)))
    for k in range(peers):
        outs[k][pl.ds(cols * ex_dev, 8), :] = tail.astype(BF16)


def pack(features, peers):
    ex_dev, modules, feat = features.shape
    shape = jax.ShapeDtypeStruct((feat // LANES * ex_dev + 8, LANES), BF16)
    outs = pl.pallas_call(
        functools.partial(pack_kernel, peers),
        out_shape=[shape] * peers,
        in_specs=[VMEM],
        out_specs=[VMEM] * peers,
        compiler_params=limit(8),
        name="pack",
    )(features)
    return dict(zip(ORDER, outs))


def pick_kernel(pool, ids, out):
    rows, queries = pool.shape[0] * pool.shape[1], ids.shape[1]
    local = lax.axis_index("row") * lax.axis_size("pb") + lax.axis_index("pb")
    wanted = ids[...] * pool.shape[1] + local
    r = lax.broadcasted_iota(jnp.int32, (rows, queries), 0)
    chosen = (r == wanted).astype(F32).astype(BF16)
    flat = pool[...].reshape(rows, pool.shape[2])
    out[...] = dot(chosen, flat, ((0,), (0,))).astype(BF16)


def pick(query_pool, ids):
    return pl.pallas_call(
        pick_kernel,
        out_shape=jax.ShapeDtypeStruct((ids.shape[1], query_pool.shape[2]), BF16),
        in_specs=[VMEM, VMEM],
        out_specs=VMEM,
        compiler_params=limit(12),
        name="pick",
    )(query_pool, ids)


def score_kernel(modules, *refs):
    peers = len(refs) - 4
    chunks, (picked, own, other, feats) = refs[:peers], refs[peers:]
    count, feat = feats.shape
    ex_dev = count // peers
    cols = feat // LANES
    total = jnp.zeros((1, LANES), F32)
    for k, chunk in zip(ORDER, chunks):
        for j in range(cols):
            feats[k * ex_dev : (k + 1) * ex_dev, j * LANES : (j + 1) * LANES] = chunk[j * ex_dev : (j + 1) * ex_dev, :]
        total = total + chunk[cols * ex_dev :, :].astype(F32).sum(0, keepdims=True)
    damping = jnp.sum(total, keepdims=True) * (0.5 / (count * modules * feat))
    f = feats[...]
    gram = dot(f, f, ((0,), (0,)))
    diag = lax.broadcasted_iota(jnp.int32, (feat, feat), 0) == lax.broadcasted_iota(jnp.int32, (feat, feat), 1)
    hessian = gram * (1.0 / count) + jnp.where(diag, damping, 0.0)
    square = jnp.sum(jnp.sum(hessian * hessian, axis=0, keepdims=True), axis=1, keepdims=True)
    inv = 1.0 / jnp.sqrt(square + 1e-06)
    high, low = split(hessian)

    def apply(v, mat):
        vh, vl = split(v)
        mh, ml = mat
        return dot(vh, mh, PLAIN) + (dot(vl, mh, PLAIN) + dot(vh, ml, PLAIN))

    v = picked[...]
    b2 = inv * (2.0 * hessian - inv * dot(high, high, PLAIN))
    m2 = split(b2)
    v = 2.0 * v.astype(F32) - inv * (dot(v, high, PLAIN) + dot(v, low, PLAIN))
    b4 = 2.0 * b2 - dot(m2[0], m2[0], PLAIN)
    m4 = split(b4)
    v = 2.0 * v - apply(v, m2)
    v = 2.0 * v - apply(v, m4)
    w = v - apply(v, m4)
    w = w - apply(w, m4)
    precond = ((v + w) * inv).astype(BF16)
    half = precond.shape[0] // 2
    scores = dot(f, precond, ((1,), (1,)))
    other[...] = scores[:, half:]
    own[...] = scores[:, :half]


def score(chunks, picked, modules):
    peers = len(chunks)
    queries, feat = picked.shape
    count = peers * (chunks[0].shape[0] - 8) * LANES // feat
    half = jax.ShapeDtypeStruct((count, queries // 2), F32)
    return pl.pallas_call(
        functools.partial(score_kernel, modules),
        out_shape=[half, half],
        in_specs=[VMEM] * (peers + 1),
        out_specs=[VMEM, VMEM],
        scratch_shapes=[pltpu.VMEM((count, feat), BF16)],
        compiler_params=limit(24),
        name="score",
    )(*chunks, picked)


def exchange(x, axes, k, size):
    return lax.ppermute(x, axes, [(i, i ^ k) for i in range(size)])


def owned(features, query_pool, query_ids):
    ex_dev, modules, feat = features.shape
    peers = lax.axis_size("gx") * lax.axis_size("row")
    ids = jnp.concatenate([query_ids, exchange(query_ids, "pb", 1, 2)])[None, :]
    chunks = pack(features, peers)
    for k in ORDER[:-1]:
        chunks[k] = exchange(chunks[k], GROUP, k, peers)
    chunks = [chunks[k] for k in ORDER]
    picked = pick(query_pool, ids)
    own, other = score(chunks, picked, modules)
    part = own + exchange(other, "pb", 1, 2)
    part = part.reshape(2, 4, ex_dev, -1)
    near = part[:, 0]
    for k in NEAR:
        near = near + exchange(part[:, k].astype(BF16), GROUP, k, peers).astype(F32)
    return near[0] + exchange(near[1].astype(BF16), GROUP, 4, peers).astype(F32)


def regrouped(features, query_pool, query_ids):
    ex_dev, modules, feat = features.shape
    regrouped = lax.all_to_all(features, "gx", split_axis=1, concat_axis=0, tiled=True)
    count = regrouped.shape[0] * lax.axis_size("row")
    grams = jnp.einsum("emk,emj->mkj", regrouped, regrouped, preferred_element_type=jnp.float32)
    grams = lax.psum(grams, "row")
    total = lax.psum(jnp.sum(jnp.trace(grams, axis1=1, axis2=2)), "gx")
    damping = 0.5 * total / (count * modules * feat)
    identity = jnp.eye(feat, dtype=jnp.float32)
    hessian = grams / count + damping * identity
    frob = jnp.sqrt(jnp.sum(hessian * hessian, axis=(1, 2)) + 1e-06)
    inverse = identity[None] / frob[:, None, None]
    for step in range(ITERS):
        product = jnp.matmul(hessian, inverse, precision=lax.Precision.HIGHEST)
        inverse = 2.0 * inverse - jnp.matmul(inverse, product, precision=lax.Precision.HIGHEST)
    picked = jnp.take(query_pool, query_ids, axis=0)
    precond = jnp.einsum(
        "qmk,mkj->qmj", picked.astype(jnp.float32), inverse, precision=lax.Precision.HIGHEST
    ).astype(jnp.bfloat16)
    local_queries = precond.shape[0]
    flat_query = precond.reshape(local_queries, -1)
    return lax.psum_scatter(
        jnp.einsum(
            "ea,qa->eq",
            regrouped.reshape(ex_dev * lax.axis_size("gx"), -1),
            flat_query,
            preferred_element_type=jnp.float32,
        ),
        "gx",
        scatter_dimension=0,
        tiled=True,
    )


def shards(features, query_pool, query_ids):
    modules = features.shape[1]
    gx, row, pb = (lax.axis_size(name) for name in ("gx", "row", "pb"))
    if (gx, row, pb) == (4, 2, 2) and modules == gx * row * pb:
        return owned(features, query_pool, query_ids)
    return regrouped(features, query_pool, query_ids)


def solution(mesh):
    in_specs = (P(("grp", "gx", "row"), None, None), P(None, "gx", None), P("pb"))
    out_specs = P(("grp", "gx", "row"), "pb")
    return jax.shard_map(shards, mesh=mesh, in_specs=in_specs, out_specs=out_specs, check_vma=False)
```

```python
import functools

import jax
import jax.numpy as jnp
from jax import lax
from jax.experimental import pallas as pl
from jax.experimental.pallas import tpu as pltpu
from jax.sharding import PartitionSpec as P

ITERS = 4
BF16 = jnp.bfloat16
F32 = jnp.float32
LANES = 128
GROUP = ("gx", "row")
VMEM = pl.BlockSpec(memory_space=pltpu.VMEM)
ORDER = (6, 5, 7, 4, 3, 2, 1, 0)
LATE = (4, 1)
NEAR = (2, 3, 1)
PLAIN = ((1,), (0,))


def limit(mib):
    return pltpu.CompilerParams(vmem_limit_bytes=mib << 20)


def dot(a, b, dims):
    return lax.dot_general(a, b, (dims, ((), ())), preferred_element_type=F32)


def split(a):
    high = a.astype(BF16)
    return high, (a - high.astype(F32)).astype(BF16)


def pack_kernel(peers, feats, *ordered):
    outs = dict(zip(ORDER, ordered))
    ex_dev, modules, feat = feats.shape
    cols = feat // LANES
    step = 256 // modules
    me = lax.axis_index("gx") * lax.axis_size("row") + lax.axis_index("row")
    side = lax.axis_index("pb")
    r = lax.broadcasted_iota(jnp.int32, (peers * step, step * modules), 0)
    c = lax.broadcasted_iota(jnp.int32, (peers * step, step * modules), 1)
    wanted = ((r // step) ^ me) * lax.axis_size("pb") + side
    pick = ((c // modules == r % step) & (c % modules == wanted)).astype(F32).astype(BF16)

    acc = jnp.zeros((8, feat), F32)
    for b in range(ex_dev // step):
        x = feats[b * step : (b + 1) * step].reshape(step * modules, feat)
        y = dot(pick, x, ((1,), (0,))).astype(BF16)
        for k in range(peers):
            for j in range(cols):
                start = j * ex_dev + b * step
                outs[k][start : start + step, :] = y[k * step : (k + 1) * step, j * LANES : (j + 1) * LANES]
        xf = x.astype(F32)
        sq = xf * xf
        acc = acc + sq.reshape(step * modules // 8, 8, feat).sum(0)
    lane = acc.sum(0, keepdims=True)
    lane = sum(lane[:, j * LANES : (j + 1) * LANES] for j in range(cols))
    high, rest = split(lane)
    mid, low = split(lane - high.astype(F32))
    row = lax.broadcasted_iota(jnp.int32, (8, LANES), 0)
    high, mid, low = (jnp.broadcast_to(v.astype(F32), (8, LANES)) for v in (high, mid, low))
    tail = jnp.where(row == 0, high, jnp.where(row == 1, mid, jnp.where(row == 2, low, 0.0)))
    for k in range(peers):
        outs[k][pl.ds(cols * ex_dev, 8), :] = tail.astype(BF16)


def pack(features, peers):
    ex_dev, modules, feat = features.shape
    shape = jax.ShapeDtypeStruct((feat // LANES * ex_dev + 8, LANES), BF16)
    outs = pl.pallas_call(
        functools.partial(pack_kernel, peers),
        out_shape=[shape] * peers,
        in_specs=[VMEM],
        out_specs=[VMEM] * peers,
        compiler_params=limit(8),
        name="pack",
    )(features)
    return dict(zip(ORDER, outs))


def pick_kernel(pool, ids, out):
    rows, queries = pool.shape[0] * pool.shape[1], ids.shape[1]
    local = lax.axis_index("row") * lax.axis_size("pb") + lax.axis_index("pb")
    wanted = ids[...] * pool.shape[1] + local
    r = lax.broadcasted_iota(jnp.int32, (rows, queries), 0)
    chosen = (r == wanted).astype(F32).astype(BF16)
    flat = pool[...].reshape(rows, pool.shape[2])
    out[...] = dot(chosen, flat, ((0,), (0,))).astype(BF16)


def pick(query_pool, ids):
    return pl.pallas_call(
        pick_kernel,
        out_shape=jax.ShapeDtypeStruct((ids.shape[1], query_pool.shape[2]), BF16),
        in_specs=[VMEM, VMEM],
        out_specs=VMEM,
        compiler_params=limit(12),
        name="pick",
    )(query_pool, ids)


def assemble(chunks, feats):
    ex_dev = feats.shape[0] // len(chunks)
    cols = feats.shape[1] // LANES
    total = jnp.zeros((1, LANES), F32)
    for k, chunk in enumerate(chunks):
        for j in range(cols):
            feats[k * ex_dev : (k + 1) * ex_dev, j * LANES : (j + 1) * LANES] = chunk[j * ex_dev : (j + 1) * ex_dev, :]
        total = total + chunk[cols * ex_dev :, :].astype(F32).sum(0, keepdims=True)
    return total


def early_kernel(*refs):
    *chunks, feats, gram, total = refs
    total[...] = jnp.broadcast_to(assemble(chunks, feats), total.shape)
    f = feats[...]
    gram[...] = dot(f, f, ((0,), (0,)))


def cost(flops):
    return pl.CostEstimate(flops=int(flops), bytes_accessed=1 << 22, transcendentals=0)


def early(chunks, feat):
    count = len(chunks) * (chunks[0].shape[0] - 8) * LANES // feat
    return pl.pallas_call(
        early_kernel,
        out_shape=[
            jax.ShapeDtypeStruct((count, feat), BF16),
            jax.ShapeDtypeStruct((feat, feat), F32),
            jax.ShapeDtypeStruct((8, LANES), F32),
        ],
        in_specs=[VMEM] * len(chunks),
        out_specs=[VMEM] * 3,
        compiler_params=limit(16),
        cost_estimate=cost(2 * count * feat * feat),
        name="early",
    )(*chunks)


def score_kernel(modules, *refs):
    *chunks, early_feats, early_gram, early_total, picked, own, other, feats = refs
    ahead, feat = early_feats.shape
    count = ahead + feats.shape[0]
    total = early_total[0:1, :] + assemble(chunks, feats)
    damping = jnp.sum(total, keepdims=True) * (0.5 / (count * modules * feat))
    f = feats[...]
    gram = early_gram[...] + dot(f, f, ((0,), (0,)))
    diag = lax.broadcasted_iota(jnp.int32, (feat, feat), 0) == lax.broadcasted_iota(jnp.int32, (feat, feat), 1)
    hessian = gram * (1.0 / count) + jnp.where(diag, damping, 0.0)
    square = jnp.sum(jnp.sum(hessian * hessian, axis=0, keepdims=True), axis=1, keepdims=True)
    inv = 1.0 / jnp.sqrt(square + 1e-06)
    high, low = split(hessian)

    def apply(v, mat):
        vh, vl = split(v)
        mh, ml = mat
        return dot(vh, mh, PLAIN) + (dot(vl, mh, PLAIN) + dot(vh, ml, PLAIN))

    v = picked[...]
    b2 = inv * (2.0 * hessian - inv * dot(high, high, PLAIN))
    m2 = split(b2)
    v = 2.0 * v.astype(F32) - inv * dot(v, high, PLAIN)
    b4 = 2.0 * b2 - dot(m2[0], m2[0], PLAIN)
    m4 = split(b4)
    v = 2.0 * v - apply(v, m2)
    v = 2.0 * v - apply(v, m4)
    w = v - apply(v, m4)
    w = w - apply(w, m4)
    precond = ((v + w) * inv).astype(BF16)
    half = precond.shape[0] // 2
    for rows, block in ((slice(0, ahead), early_feats[...]), (slice(ahead, count), f)):
        scores = dot(block, precond, ((1,), (1,)))
        other[rows, :] = scores[:, half:]
        own[rows, :] = scores[:, :half]


def score(late, ahead, picked, modules):
    queries, feat = picked.shape
    late_count = len(late) * (late[0].shape[0] - 8) * LANES // feat
    count = ahead[0].shape[0] + late_count
    half = jax.ShapeDtypeStruct((count, queries // 2), F32)
    return pl.pallas_call(
        functools.partial(score_kernel, modules),
        out_shape=[half, half],
        in_specs=[VMEM] * (len(late) + 4),
        out_specs=[VMEM, VMEM],
        scratch_shapes=[pltpu.VMEM((late_count, feat), BF16)],
        compiler_params=limit(24),
        name="score",
    )(*late, *ahead, picked)


def exchange(x, axes, k, size):
    return lax.ppermute(x, axes, [(i, i ^ k) for i in range(size)])


def owned(features, query_pool, query_ids):
    ex_dev, modules, feat = features.shape
    peers = lax.axis_size("gx") * lax.axis_size("row")
    ids = jnp.concatenate([query_ids, exchange(query_ids, "pb", 1, 2)])[None, :]
    chunks = pack(features, peers)
    for k in ORDER[:-1]:
        chunks[k] = exchange(chunks[k], GROUP, k, peers)
    picked = pick(query_pool, ids)
    first = [k for k in ORDER if k not in LATE]
    ahead = early([chunks[k] for k in first], feat)
    own, other = score([chunks[k] for k in LATE], ahead, picked, modules)
    part = own + exchange(other, "pb", 1, 2)
    part = part.reshape(peers, ex_dev, -1)
    place = {k: i for i, k in enumerate(first + list(LATE))}
    pair = lambda k: jnp.stack([part[place[k]], part[place[k + 4]]])
    near = pair(0)
    for k in NEAR:
        near = near + exchange(pair(k).astype(BF16), GROUP, k, peers).astype(F32)
    return near[0] + exchange(near[1].astype(BF16), GROUP, 4, peers).astype(F32)


def regrouped(features, query_pool, query_ids):
    ex_dev, modules, feat = features.shape
    regrouped = lax.all_to_all(features, "gx", split_axis=1, concat_axis=0, tiled=True)
    count = regrouped.shape[0] * lax.axis_size("row")
    grams = jnp.einsum("emk,emj->mkj", regrouped, regrouped, preferred_element_type=jnp.float32)
    grams = lax.psum(grams, "row")
    total = lax.psum(jnp.sum(jnp.trace(grams, axis1=1, axis2=2)), "gx")
    damping = 0.5 * total / (count * modules * feat)
    identity = jnp.eye(feat, dtype=jnp.float32)
    hessian = grams / count + damping * identity
    frob = jnp.sqrt(jnp.sum(hessian * hessian, axis=(1, 2)) + 1e-06)
    inverse = identity[None] / frob[:, None, None]
    for step in range(ITERS):
        product = jnp.matmul(hessian, inverse, precision=lax.Precision.HIGHEST)
        inverse = 2.0 * inverse - jnp.matmul(inverse, product, precision=lax.Precision.HIGHEST)
    picked = jnp.take(query_pool, query_ids, axis=0)
    precond = jnp.einsum(
        "qmk,mkj->qmj", picked.astype(jnp.float32), inverse, precision=lax.Precision.HIGHEST
    ).astype(jnp.bfloat16)
    local_queries = precond.shape[0]
    flat_query = precond.reshape(local_queries, -1)
    return lax.psum_scatter(
        jnp.einsum(
            "ea,qa->eq",
            regrouped.reshape(ex_dev * lax.axis_size("gx"), -1),
            flat_query,
            preferred_element_type=jnp.float32,
        ),
        "gx",
        scatter_dimension=0,
        tiled=True,
    )


def shards(features, query_pool, query_ids):
    modules = features.shape[1]
    gx, row, pb = (lax.axis_size(name) for name in ("gx", "row", "pb"))
    if (gx, row, pb) == (4, 2, 2) and modules == gx * row * pb:
        return owned(features, query_pool, query_ids)
    return regrouped(features, query_pool, query_ids)


def solution(mesh):
    in_specs = (P(("grp", "gx", "row"), None, None), P(None, "gx", None), P("pb"))
    out_specs = P(("grp", "gx", "row"), "pb")
    return jax.shard_map(shards, mesh=mesh, in_specs=in_specs, out_specs=out_specs, check_vma=False)
```

```python
import functools

import jax
import jax.numpy as jnp
from jax import lax
from jax.experimental import pallas as pl
from jax.experimental.pallas import tpu as pltpu
from jax.sharding import PartitionSpec as P

ITERS = 4
BF16 = jnp.bfloat16
F32 = jnp.float32
LANES = 128
GROUP = ("gx", "row")
VMEM = pl.BlockSpec(memory_space=pltpu.VMEM)
ORDER = (6, 5, 7, 4, 3, 2, 1, 0)
LATE = (4, 1)
NEAR = (3, 1, 2)
PLAIN = ((1,), (0,))


def limit(mib):
    return pltpu.CompilerParams(vmem_limit_bytes=mib << 20)


def dot(a, b, dims):
    return lax.dot_general(a, b, (dims, ((), ())), preferred_element_type=F32)


def split(a):
    high = a.astype(BF16)
    return high, (a - high.astype(F32)).astype(BF16)


def pack_kernel(peers, feats, *ordered):
    outs = dict(zip(ORDER, ordered))
    ex_dev, modules, feat = feats.shape
    cols = feat // LANES
    step = 256 // modules
    me = lax.axis_index("gx") * lax.axis_size("row") + lax.axis_index("row")
    side = lax.axis_index("pb")
    r = lax.broadcasted_iota(jnp.int32, (peers * step, step * modules), 0)
    c = lax.broadcasted_iota(jnp.int32, (peers * step, step * modules), 1)
    wanted = ((r // step) ^ me) * lax.axis_size("pb") + side
    pick = ((c // modules == r % step) & (c % modules == wanted)).astype(F32).astype(BF16)

    acc = jnp.zeros((8, feat), F32)
    for b in range(ex_dev // step):
        x = feats[b * step : (b + 1) * step].reshape(step * modules, feat)
        y = dot(pick, x, ((1,), (0,))).astype(BF16)
        for k in range(peers):
            for j in range(cols):
                start = j * ex_dev + b * step
                outs[k][start : start + step, :] = y[k * step : (k + 1) * step, j * LANES : (j + 1) * LANES]
        xf = x.astype(F32)
        sq = xf * xf
        acc = acc + sq.reshape(step * modules // 8, 8, feat).sum(0)
    lane = acc.sum(0, keepdims=True)
    lane = sum(lane[:, j * LANES : (j + 1) * LANES] for j in range(cols))
    high, rest = split(lane)
    mid, low = split(lane - high.astype(F32))
    row = lax.broadcasted_iota(jnp.int32, (8, LANES), 0)
    high, mid, low = (jnp.broadcast_to(v.astype(F32), (8, LANES)) for v in (high, mid, low))
    tail = jnp.where(row == 0, high, jnp.where(row == 1, mid, jnp.where(row == 2, low, 0.0)))
    for k in range(peers):
        outs[k][pl.ds(cols * ex_dev, 8), :] = tail.astype(BF16)


def pack(features, peers):
    ex_dev, modules, feat = features.shape
    shape = jax.ShapeDtypeStruct((feat // LANES * ex_dev + 8, LANES), BF16)
    outs = pl.pallas_call(
        functools.partial(pack_kernel, peers),
        out_shape=[shape] * peers,
        in_specs=[VMEM],
        out_specs=[VMEM] * peers,
        compiler_params=limit(8),
        name="pack",
    )(features)
    return dict(zip(ORDER, outs))


def pick_kernel(pool, ids, out):
    rows, queries = pool.shape[0] * pool.shape[1], ids.shape[1]
    local = lax.axis_index("row") * lax.axis_size("pb") + lax.axis_index("pb")
    wanted = ids[...] * pool.shape[1] + local
    r = lax.broadcasted_iota(jnp.int32, (rows, queries), 0)
    chosen = (r == wanted).astype(F32).astype(BF16)
    flat = pool[...].reshape(rows, pool.shape[2])
    out[...] = dot(chosen, flat, ((0,), (0,))).astype(BF16)


def pick(query_pool, ids):
    return pl.pallas_call(
        pick_kernel,
        out_shape=jax.ShapeDtypeStruct((ids.shape[1], query_pool.shape[2]), BF16),
        in_specs=[VMEM, VMEM],
        out_specs=VMEM,
        compiler_params=limit(12),
        name="pick",
    )(query_pool, ids)


def assemble(chunks, feats):
    ex_dev = feats.shape[0] // len(chunks)
    cols = feats.shape[1] // LANES
    total = jnp.zeros((1, LANES), F32)
    for k, chunk in enumerate(chunks):
        for j in range(cols):
            feats[k * ex_dev : (k + 1) * ex_dev, j * LANES : (j + 1) * LANES] = chunk[j * ex_dev : (j + 1) * ex_dev, :]
        total = total + chunk[cols * ex_dev :, :].astype(F32).sum(0, keepdims=True)
    return total


def early_kernel(*refs):
    *chunks, feats, gram, total = refs
    total[...] = jnp.broadcast_to(assemble(chunks, feats), total.shape)
    f = feats[...]
    gram[...] = dot(f, f, ((0,), (0,)))


def cost(flops):
    return pl.CostEstimate(flops=int(flops), bytes_accessed=1 << 22, transcendentals=0)


def early(chunks, feat):
    count = len(chunks) * (chunks[0].shape[0] - 8) * LANES // feat
    return pl.pallas_call(
        early_kernel,
        out_shape=[
            jax.ShapeDtypeStruct((count, feat), BF16),
            jax.ShapeDtypeStruct((feat, feat), F32),
            jax.ShapeDtypeStruct((8, LANES), F32),
        ],
        in_specs=[VMEM] * len(chunks),
        out_specs=[VMEM] * 3,
        compiler_params=limit(16),
        cost_estimate=cost(2 * count * feat * feat),
        name="early",
    )(*chunks)


def score_kernel(modules, *refs):
    *chunks, early_feats, early_gram, early_total, picked, own, other, feats = refs
    ahead, feat = early_feats.shape
    count = ahead + feats.shape[0]
    total = early_total[0:1, :] + assemble(chunks, feats)
    damping = jnp.sum(total, keepdims=True) * (0.5 / (count * modules * feat))
    f = feats[...]
    gram = early_gram[...] + dot(f, f, ((0,), (0,)))
    diag = lax.broadcasted_iota(jnp.int32, (feat, feat), 0) == lax.broadcasted_iota(jnp.int32, (feat, feat), 1)
    hessian = gram * (1.0 / count) + jnp.where(diag, damping, 0.0)
    square = jnp.sum(jnp.sum(hessian * hessian, axis=0, keepdims=True), axis=1, keepdims=True)
    inv = 1.0 / jnp.sqrt(square + 1e-06)
    high, low = split(hessian)

    def apply(v, mat):
        vh, vl = split(v)
        mh, ml = mat
        return dot(vh, mh, PLAIN) + (dot(vl, mh, PLAIN) + dot(vh, ml, PLAIN))

    v = picked[...]
    b2 = inv * (2.0 * hessian - inv * dot(high, high, PLAIN))
    m2 = split(b2)
    v = 2.0 * v.astype(F32) - inv * dot(v, high, PLAIN)
    b4 = 2.0 * b2 - dot(m2[0], m2[0], PLAIN)
    m4 = split(b4)
    b8 = 2.0 * b4 - dot(m4[0], m4[0], PLAIN)
    m8 = split(b8)
    vh = v.astype(BF16)
    v = 2.0 * v - (dot(vh, m2[0], PLAIN) + dot(vh, m2[1], PLAIN))
    v = 2.0 * v - apply(v, m4)
    v = 2.0 * v - apply(v, m8)
    precond = (v * inv).astype(BF16)
    half = precond.shape[0] // 2
    for rows, block in ((slice(0, ahead), early_feats[...]), (slice(ahead, count), f)):
        scores = dot(block, precond, ((1,), (1,)))
        other[rows, :] = scores[:, half:].astype(BF16)
        own[rows, :] = scores[:, :half]


def score(late, ahead, picked, modules):
    queries, feat = picked.shape
    late_count = len(late) * (late[0].shape[0] - 8) * LANES // feat
    count = ahead[0].shape[0] + late_count
    half = jax.ShapeDtypeStruct((count, queries // 2), F32)
    sent = jax.ShapeDtypeStruct(half.shape, BF16)
    return pl.pallas_call(
        functools.partial(score_kernel, modules),
        out_shape=[half, sent],
        in_specs=[VMEM] * (len(late) + 4),
        out_specs=[VMEM, VMEM],
        scratch_shapes=[pltpu.VMEM((late_count, feat), BF16)],
        compiler_params=limit(24),
        name="score",
    )(*late, *ahead, picked)


def exchange(x, axes, k, size):
    return lax.ppermute(x, axes, [(i, i ^ k) for i in range(size)])


def owned(features, query_pool, query_ids):
    ex_dev, modules, feat = features.shape
    peers = lax.axis_size("gx") * lax.axis_size("row")
    ids = jnp.concatenate([query_ids, exchange(query_ids, "pb", 1, 2)])[None, :]
    chunks = pack(features, peers)
    for k in ORDER[:-1]:
        chunks[k] = exchange(chunks[k], GROUP, k, peers)
    picked = pick(query_pool, ids)
    first = [k for k in ORDER if k not in LATE]
    ahead = early([chunks[k] for k in first], feat)
    own, other = score([chunks[k] for k in LATE], ahead, picked, modules)
    part = own + exchange(other, "pb", 1, 2).astype(F32)
    part = part.reshape(peers, ex_dev, -1)
    place = {k: i for i, k in enumerate(first + list(LATE))}
    pair = lambda k: jnp.stack([part[place[k]], part[place[k + 4]]])
    near = pair(0)
    for k in NEAR:
        near = near + exchange(pair(k).astype(BF16), GROUP, k, peers).astype(F32)
    return near[0] + exchange(near[1].astype(BF16), GROUP, 4, peers).astype(F32)


def regrouped(features, query_pool, query_ids):
    ex_dev, modules, feat = features.shape
    regrouped = lax.all_to_all(features, "gx", split_axis=1, concat_axis=0, tiled=True)
    count = regrouped.shape[0] * lax.axis_size("row")
    grams = jnp.einsum("emk,emj->mkj", regrouped, regrouped, preferred_element_type=jnp.float32)
    grams = lax.psum(grams, "row")
    total = lax.psum(jnp.sum(jnp.trace(grams, axis1=1, axis2=2)), "gx")
    damping = 0.5 * total / (count * modules * feat)
    identity = jnp.eye(feat, dtype=jnp.float32)
    hessian = grams / count + damping * identity
    frob = jnp.sqrt(jnp.sum(hessian * hessian, axis=(1, 2)) + 1e-06)
    inverse = identity[None] / frob[:, None, None]
    for step in range(ITERS):
        product = jnp.matmul(hessian, inverse, precision=lax.Precision.HIGHEST)
        inverse = 2.0 * inverse - jnp.matmul(inverse, product, precision=lax.Precision.HIGHEST)
    picked = jnp.take(query_pool, query_ids, axis=0)
    precond = jnp.einsum(
        "qmk,mkj->qmj", picked.astype(jnp.float32), inverse, precision=lax.Precision.HIGHEST
    ).astype(jnp.bfloat16)
    local_queries = precond.shape[0]
    flat_query = precond.reshape(local_queries, -1)
    return lax.psum_scatter(
        jnp.einsum(
            "ea,qa->eq",
            regrouped.reshape(ex_dev * lax.axis_size("gx"), -1),
            flat_query,
            preferred_element_type=jnp.float32,
        ),
        "gx",
        scatter_dimension=0,
        tiled=True,
    )


def shards(features, query_pool, query_ids):
    modules = features.shape[1]
    gx, row, pb = (lax.axis_size(name) for name in ("gx", "row", "pb"))
    if (gx, row, pb) == (4, 2, 2) and modules == gx * row * pb:
        return owned(features, query_pool, query_ids)
    return regrouped(features, query_pool, query_ids)


def solution(mesh):
    in_specs = (P(("grp", "gx", "row"), None, None), P(None, "gx", None), P("pb"))
    out_specs = P(("grp", "gx", "row"), "pb")
    return jax.shard_map(shards, mesh=mesh, in_specs=in_specs, out_specs=out_specs, check_vma=False)
```

```python
import functools

import jax
import jax.numpy as jnp
from jax import lax
from jax.experimental import pallas as pl
from jax.experimental.pallas import tpu as pltpu
from jax.sharding import PartitionSpec as P

ITERS = 4
BF16 = jnp.bfloat16
F32 = jnp.float32
LANES = 128
GROUP = ("gx", "row")
VMEM = pl.BlockSpec(memory_space=pltpu.VMEM)
ORDER = (6, 1, 5, 7, 4, 3, 2, 0)
LATE = (4, 1)
AHEAD = tuple(k for k in ORDER if k not in LATE)
NEAR = (2, 3, 1)
PLAIN = ((1,), (0,))


def limit(mib):
    return pltpu.CompilerParams(vmem_limit_bytes=mib << 20)


def dot(a, b, dims):
    return lax.dot_general(a, b, (dims, ((), ())), preferred_element_type=F32)


def split(a):
    high = a.astype(BF16)
    return high, (a - high.astype(F32)).astype(BF16)


def pack_kernel(peers, feats, *ordered):
    outs = dict(zip(ORDER, ordered))
    ex_dev, modules, feat = feats.shape
    cols = feat // LANES
    step = 256 // modules
    me = lax.axis_index("gx") * lax.axis_size("row") + lax.axis_index("row")
    side = lax.axis_index("pb")
    r = lax.broadcasted_iota(jnp.int32, (peers * step, step * modules), 0)
    c = lax.broadcasted_iota(jnp.int32, (peers * step, step * modules), 1)
    wanted = ((r // step) ^ me) * lax.axis_size("pb") + side
    pick = ((c // modules == r % step) & (c % modules == wanted)).astype(F32).astype(BF16)

    acc = jnp.zeros((8, feat), F32)
    for b in range(ex_dev // step):
        x = feats[b * step : (b + 1) * step].reshape(step * modules, feat)
        y = dot(pick, x, ((1,), (0,))).astype(BF16)
        for k in range(peers):
            for j in range(cols):
                start = j * ex_dev + b * step
                outs[k][start : start + step, :] = y[k * step : (k + 1) * step, j * LANES : (j + 1) * LANES]
        xf = x.astype(F32)
        sq = xf * xf
        acc = acc + sq.reshape(step * modules // 8, 8, feat).sum(0)
    lane = acc.sum(0, keepdims=True)
    lane = sum(lane[:, j * LANES : (j + 1) * LANES] for j in range(cols))
    high, rest = split(lane)
    mid, low = split(lane - high.astype(F32))
    row = lax.broadcasted_iota(jnp.int32, (8, LANES), 0)
    high, mid, low = (jnp.broadcast_to(v.astype(F32), (8, LANES)) for v in (high, mid, low))
    tail = jnp.where(row == 0, high, jnp.where(row == 1, mid, jnp.where(row == 2, low, 0.0)))
    for k in range(peers):
        outs[k][pl.ds(cols * ex_dev, 8), :] = tail.astype(BF16)


def pack(features, peers):
    ex_dev, modules, feat = features.shape
    shape = jax.ShapeDtypeStruct((feat // LANES * ex_dev + 8, LANES), BF16)
    outs = pl.pallas_call(
        functools.partial(pack_kernel, peers),
        out_shape=[shape] * peers,
        in_specs=[VMEM],
        out_specs=[VMEM] * peers,
        compiler_params=limit(8),
        name="pack",
    )(features)
    return dict(zip(ORDER, outs))


def pick_kernel(pool, ids, out):
    rows, queries = pool.shape[0] * pool.shape[1], ids.shape[1]
    local = lax.axis_index("row") * lax.axis_size("pb") + lax.axis_index("pb")
    wanted = ids[...] * pool.shape[1] + local
    r = lax.broadcasted_iota(jnp.int32, (rows, queries), 0)
    chosen = (r == wanted).astype(F32).astype(BF16)
    flat = pool[...].reshape(rows, pool.shape[2])
    out[...] = dot(chosen, flat, ((0,), (0,))).astype(BF16)


def pick(query_pool, ids):
    return pl.pallas_call(
        pick_kernel,
        out_shape=jax.ShapeDtypeStruct((ids.shape[1], query_pool.shape[2]), BF16),
        in_specs=[VMEM, VMEM],
        out_specs=VMEM,
        compiler_params=limit(12),
        name="pick",
    )(query_pool, ids)


def assemble(chunks, feats):
    ex_dev = feats.shape[0] // len(chunks)
    cols = feats.shape[1] // LANES
    total = jnp.zeros((1, LANES), F32)
    for k, chunk in enumerate(chunks):
        for j in range(cols):
            feats[k * ex_dev : (k + 1) * ex_dev, j * LANES : (j + 1) * LANES] = chunk[j * ex_dev : (j + 1) * ex_dev, :]
        total = total + chunk[cols * ex_dev :, :].astype(F32).sum(0, keepdims=True)
    return total


def early_kernel(*refs):
    *chunks, feats, gram, total = refs
    total[...] = jnp.broadcast_to(assemble(chunks, feats), total.shape)
    f = feats[...]
    gram[...] = dot(f, f, ((0,), (0,)))


def cost(flops):
    return pl.CostEstimate(flops=int(flops), bytes_accessed=1 << 22, transcendentals=0)


def early(chunks, feat):
    count = len(chunks) * (chunks[0].shape[0] - 8) * LANES // feat
    return pl.pallas_call(
        early_kernel,
        out_shape=[
            jax.ShapeDtypeStruct((count, feat), BF16),
            jax.ShapeDtypeStruct((feat, feat), F32),
            jax.ShapeDtypeStruct((8, LANES), F32),
        ],
        in_specs=[VMEM] * len(chunks),
        out_specs=[VMEM] * 3,
        compiler_params=limit(16),
        cost_estimate=cost(2 * count * feat * feat),
        name="early",
    )(*chunks)


def score_kernel(modules, *refs):
    *chunks, early_feats, early_gram, early_total, picked, own, other, feats = refs
    ahead, feat = early_feats.shape
    count = ahead + feats.shape[0]
    total = early_total[0:1, :] + assemble(chunks, feats)
    damping = jnp.sum(total, keepdims=True) * (0.5 / (count * modules * feat))
    f = feats[...]
    gram = early_gram[...] + dot(f, f, ((0,), (0,)))
    diag = lax.broadcasted_iota(jnp.int32, (feat, feat), 0) == lax.broadcasted_iota(jnp.int32, (feat, feat), 1)
    hessian = gram * (1.0 / count) + jnp.where(diag, damping, 0.0)
    square = jnp.sum(jnp.sum(hessian * hessian, axis=0, keepdims=True), axis=1, keepdims=True)
    inv = 1.0 / jnp.sqrt(square + 1e-06)
    high, low = split(hessian)

    def apply(v, mat):
        vh, vl = split(v)
        mh, ml = mat
        return dot(vh, mh, PLAIN) + (dot(vl, mh, PLAIN) + dot(vh, ml, PLAIN))

    v = picked[...]
    b2 = inv * (2.0 * hessian - inv * dot(high, high, PLAIN))
    m2 = split(b2)
    v = 2.0 * v.astype(F32) - inv * dot(v, high, PLAIN)
    b4 = 2.0 * b2 - dot(m2[0], m2[0], PLAIN)
    m4 = split(b4)
    b8 = 2.0 * b4 - dot(m4[0], m4[0], PLAIN)
    m8 = split(b8)
    vh = v.astype(BF16)
    v = 2.0 * v - (dot(vh, m2[0], PLAIN) + dot(vh, m2[1], PLAIN))
    v = 2.0 * v - apply(v, m4)
    v = 2.0 * v - apply(v, m8)
    precond = (v * inv).astype(BF16)
    half = precond.shape[0] // 2
    ex_dev = feats.shape[0] // len(LATE)
    for keys, block in ((AHEAD, early_feats[...]), (LATE, f)):
        scores = dot(block, precond, ((1,), (1,)))
        for i, k in enumerate(keys):
            rows = scores[i * ex_dev : (i + 1) * ex_dev]
            other[k % 4, k // 4] = rows[:, half:].astype(BF16)
            own[k % 4, k // 4] = rows[:, :half]


def score(late, ahead, picked, modules):
    queries, feat = picked.shape
    late_count = len(late) * (late[0].shape[0] - 8) * LANES // feat
    block = (4, 2, late_count // len(late), queries // 2)
    return pl.pallas_call(
        functools.partial(score_kernel, modules),
        out_shape=[jax.ShapeDtypeStruct(block, F32), jax.ShapeDtypeStruct(block, BF16)],
        in_specs=[VMEM] * (len(late) + 4),
        out_specs=[VMEM, VMEM],
        scratch_shapes=[pltpu.VMEM((late_count, feat), BF16)],
        compiler_params=limit(24),
        name="score",
    )(*late, *ahead, picked)


def exchange(x, axes, k, size):
    return lax.ppermute(x, axes, [(i, i ^ k) for i in range(size)])


def owned(features, query_pool, query_ids):
    ex_dev, modules, feat = features.shape
    peers = lax.axis_size("gx") * lax.axis_size("row")
    ids = jnp.concatenate([query_ids, exchange(query_ids, "pb", 1, 2)])[None, :]
    chunks = pack(features, peers)
    for k in ORDER[:-1]:
        chunks[k] = exchange(chunks[k], GROUP, k, peers)
    picked = pick(query_pool, ids)
    ahead = early([chunks[k] for k in AHEAD], feat)
    own, other = score([chunks[k] for k in LATE], ahead, picked, modules)
    part = own + exchange(other, "pb", 1, 2).astype(F32)
    near = part[0]
    for k in NEAR:
        near = near + exchange(part[k].astype(BF16), GROUP, k, peers).astype(F32)
    return near[0] + exchange(near[1].astype(BF16), GROUP, 4, peers).astype(F32)


def regrouped(features, query_pool, query_ids):
    ex_dev, modules, feat = features.shape
    regrouped = lax.all_to_all(features, "gx", split_axis=1, concat_axis=0, tiled=True)
    count = regrouped.shape[0] * lax.axis_size("row")
    grams = jnp.einsum("emk,emj->mkj", regrouped, regrouped, preferred_element_type=jnp.float32)
    grams = lax.psum(grams, "row")
    total = lax.psum(jnp.sum(jnp.trace(grams, axis1=1, axis2=2)), "gx")
    damping = 0.5 * total / (count * modules * feat)
    identity = jnp.eye(feat, dtype=jnp.float32)
    hessian = grams / count + damping * identity
    frob = jnp.sqrt(jnp.sum(hessian * hessian, axis=(1, 2)) + 1e-06)
    inverse = identity[None] / frob[:, None, None]
    for step in range(ITERS):
        product = jnp.matmul(hessian, inverse, precision=lax.Precision.HIGHEST)
        inverse = 2.0 * inverse - jnp.matmul(inverse, product, precision=lax.Precision.HIGHEST)
    picked = jnp.take(query_pool, query_ids, axis=0)
    precond = jnp.einsum(
        "qmk,mkj->qmj", picked.astype(jnp.float32), inverse, precision=lax.Precision.HIGHEST
    ).astype(jnp.bfloat16)
    local_queries = precond.shape[0]
    flat_query = precond.reshape(local_queries, -1)
    return lax.psum_scatter(
        jnp.einsum(
            "ea,qa->eq",
            regrouped.reshape(ex_dev * lax.axis_size("gx"), -1),
            flat_query,
            preferred_element_type=jnp.float32,
        ),
        "gx",
        scatter_dimension=0,
        tiled=True,
    )


def shards(features, query_pool, query_ids):
    modules = features.shape[1]
    gx, row, pb = (lax.axis_size(name) for name in ("gx", "row", "pb"))
    if (gx, row, pb) == (4, 2, 2) and modules == gx * row * pb:
        return owned(features, query_pool, query_ids)
    return regrouped(features, query_pool, query_ids)


def solution(mesh):
    in_specs = (P(("grp", "gx", "row"), None, None), P(None, "gx", None), P("pb"))
    out_specs = P(("grp", "gx", "row"), "pb")
    return jax.shard_map(shards, mesh=mesh, in_specs=in_specs, out_specs=out_specs, check_vma=False)
```

```python
import functools

import jax
import jax.numpy as jnp
from jax import lax
from jax.experimental import pallas as pl
from jax.experimental.pallas import tpu as pltpu
from jax.sharding import PartitionSpec as P

ITERS = 4
BF16 = jnp.bfloat16
F32 = jnp.float32
LANES = 128
GROUP = ("gx", "row")
VMEM = pl.BlockSpec(memory_space=pltpu.VMEM)
ORDER = (6, 1, 5, 7, 4, 3, 2, 0)
LATE = (4, 1)
AHEAD = tuple(k for k in ORDER if k not in LATE)
NEAR = (2, 3, 1)
PLAIN = ((1,), (0,))


def limit(mib):
    return pltpu.CompilerParams(vmem_limit_bytes=mib << 20)


def dot(a, b, dims):
    return lax.dot_general(a, b, (dims, ((), ())), preferred_element_type=F32)


def split(a):
    high = a.astype(BF16)
    return high, (a - high.astype(F32)).astype(BF16)


def pack_kernel(peers, hbm, *refs):
    *ordered, feats, sems = refs
    outs = dict(zip(ORDER, ordered))
    half = feats.shape[0] // 2
    copies = [
        pltpu.make_async_copy(hbm.at[pl.ds(i * half, half)], feats.at[pl.ds(i * half, half)], sems.at[i])
        for i in range(2)
    ]
    for copy in copies:
        copy.start()
    ex_dev, modules, feat = feats.shape
    cols = feat // LANES
    step = 256 // modules
    me = lax.axis_index("gx") * lax.axis_size("row") + lax.axis_index("row")
    side = lax.axis_index("pb")
    r = lax.broadcasted_iota(jnp.int32, (peers * step, step * modules), 0)
    c = lax.broadcasted_iota(jnp.int32, (peers * step, step * modules), 1)
    wanted = ((r // step) ^ me) * lax.axis_size("pb") + side
    pick = ((c // modules == r % step) & (c % modules == wanted)).astype(F32).astype(BF16)

    acc = jnp.zeros((8, feat), F32)
    for b in range(ex_dev // step):
        if b * step % half == 0:
            copies[b * step // half].wait()
        x = feats[b * step : (b + 1) * step].reshape(step * modules, feat)
        y = dot(pick, x, ((1,), (0,))).astype(BF16)
        for k in range(peers):
            for j in range(cols):
                start = j * ex_dev + b * step
                outs[k][start : start + step, :] = y[k * step : (k + 1) * step, j * LANES : (j + 1) * LANES]
        xf = x.astype(F32)
        sq = xf * xf
        acc = acc + sq.reshape(step * modules // 8, 8, feat).sum(0)
    lane = acc.sum(0, keepdims=True)
    lane = sum(lane[:, j * LANES : (j + 1) * LANES] for j in range(cols))
    high, rest = split(lane)
    mid, low = split(lane - high.astype(F32))
    row = lax.broadcasted_iota(jnp.int32, (8, LANES), 0)
    high, mid, low = (jnp.broadcast_to(v.astype(F32), (8, LANES)) for v in (high, mid, low))
    tail = jnp.where(row == 0, high, jnp.where(row == 1, mid, jnp.where(row == 2, low, 0.0)))
    for k in range(peers):
        outs[k][pl.ds(cols * ex_dev, 8), :] = tail.astype(BF16)


def pack(features, peers):
    ex_dev, modules, feat = features.shape
    shape = jax.ShapeDtypeStruct((feat // LANES * ex_dev + 8, LANES), BF16)
    outs = pl.pallas_call(
        functools.partial(pack_kernel, peers),
        out_shape=[shape] * peers,
        in_specs=[pl.BlockSpec(memory_space=pltpu.HBM)],
        out_specs=[VMEM] * peers,
        scratch_shapes=[pltpu.VMEM(features.shape, BF16), pltpu.SemaphoreType.DMA((2,))],
        compiler_params=limit(8),
        name="pack",
    )(pltpu.with_memory_space_constraint(features, pltpu.HBM))
    return dict(zip(ORDER, outs))


def pick_kernel(pool, ids, out):
    rows, queries = pool.shape[0] * pool.shape[1], ids.shape[1]
    local = lax.axis_index("row") * lax.axis_size("pb") + lax.axis_index("pb")
    wanted = ids[...] * pool.shape[1] + local
    r = lax.broadcasted_iota(jnp.int32, (rows, queries), 0)
    chosen = (r == wanted).astype(F32).astype(BF16)
    flat = pool[...].reshape(rows, pool.shape[2])
    out[...] = dot(chosen, flat, ((0,), (0,))).astype(BF16)


def pick(query_pool, ids):
    return pl.pallas_call(
        pick_kernel,
        out_shape=jax.ShapeDtypeStruct((ids.shape[1], query_pool.shape[2]), BF16),
        in_specs=[VMEM, VMEM],
        out_specs=VMEM,
        compiler_params=limit(12),
        name="pick",
    )(query_pool, ids)


def assemble(chunks, feats):
    ex_dev = feats.shape[0] // len(chunks)
    cols = feats.shape[1] // LANES
    total = jnp.zeros((1, LANES), F32)
    for k, chunk in enumerate(chunks):
        for j in range(cols):
            feats[k * ex_dev : (k + 1) * ex_dev, j * LANES : (j + 1) * LANES] = chunk[j * ex_dev : (j + 1) * ex_dev, :]
        total = total + chunk[cols * ex_dev :, :].astype(F32).sum(0, keepdims=True)
    return total


def early_kernel(*refs):
    *chunks, feats, gram, total = refs
    total[...] = jnp.broadcast_to(assemble(chunks, feats), total.shape)
    f = feats[...]
    gram[...] = dot(f, f, ((0,), (0,)))


def cost(flops):
    return pl.CostEstimate(flops=int(flops), bytes_accessed=1 << 22, transcendentals=0)


def early(chunks, feat):
    count = len(chunks) * (chunks[0].shape[0] - 8) * LANES // feat
    return pl.pallas_call(
        early_kernel,
        out_shape=[
            jax.ShapeDtypeStruct((count, feat), BF16),
            jax.ShapeDtypeStruct((feat, feat), F32),
            jax.ShapeDtypeStruct((8, LANES), F32),
        ],
        in_specs=[VMEM] * len(chunks),
        out_specs=[VMEM] * 3,
        compiler_params=limit(16),
        cost_estimate=cost(2 * count * feat * feat),
        name="early",
    )(*chunks)


def score_kernel(modules, *refs):
    *chunks, early_feats, early_gram, early_total, picked, own, other, feats = refs
    ahead, feat = early_feats.shape
    count = ahead + feats.shape[0]
    total = early_total[0:1, :] + assemble(chunks, feats)
    damping = jnp.sum(total, keepdims=True) * (0.5 / (count * modules * feat))
    f = feats[...]
    gram = early_gram[...] + dot(f, f, ((0,), (0,)))
    diag = lax.broadcasted_iota(jnp.int32, (feat, feat), 0) == lax.broadcasted_iota(jnp.int32, (feat, feat), 1)
    hessian = gram * (1.0 / count) + jnp.where(diag, damping, 0.0)
    square = jnp.sum(jnp.sum(hessian * hessian, axis=0, keepdims=True), axis=1, keepdims=True)
    inv = 1.0 / jnp.sqrt(square + 1e-06)
    high, low = split(hessian)

    def apply(v, mat):
        vh, vl = split(v)
        mh, ml = mat
        return dot(vh, mh, PLAIN) + (dot(vl, mh, PLAIN) + dot(vh, ml, PLAIN))

    v = picked[...]
    b2 = inv * (2.0 * hessian - inv * dot(high, high, PLAIN))
    m2 = split(b2)
    v = 2.0 * v.astype(F32) - inv * dot(v, high, PLAIN)
    b4 = 2.0 * b2 - dot(m2[0], m2[0], PLAIN)
    m4 = split(b4)
    b8 = 2.0 * b4 - dot(m4[0], m4[0], PLAIN)
    m8 = split(b8)
    vh = v.astype(BF16)
    v = 2.0 * v - (dot(vh, m2[0], PLAIN) + dot(vh, m2[1], PLAIN))
    v = 2.0 * v - apply(v, m4)
    v = 2.0 * v - apply(v, m8)
    precond = (v * inv).astype(BF16)
    half = precond.shape[0] // 2
    ex_dev = feats.shape[0] // len(LATE)
    for keys, block in ((AHEAD, early_feats[...]), (LATE, f)):
        scores = dot(block, precond, ((1,), (1,)))
        for i, k in enumerate(keys):
            rows = scores[i * ex_dev : (i + 1) * ex_dev]
            other[k % 4, k // 4] = rows[:, half:].astype(BF16)
            own[k % 4, k // 4] = rows[:, :half]


def score(late, ahead, picked, modules):
    queries, feat = picked.shape
    late_count = len(late) * (late[0].shape[0] - 8) * LANES // feat
    block = (4, 2, late_count // len(late), queries // 2)
    return pl.pallas_call(
        functools.partial(score_kernel, modules),
        out_shape=[jax.ShapeDtypeStruct(block, F32), jax.ShapeDtypeStruct(block, BF16)],
        in_specs=[VMEM] * (len(late) + 4),
        out_specs=[VMEM, VMEM],
        scratch_shapes=[pltpu.VMEM((late_count, feat), BF16)],
        compiler_params=limit(24),
        name="score",
    )(*late, *ahead, picked)


def exchange(x, axes, k, size):
    return lax.ppermute(x, axes, [(i, i ^ k) for i in range(size)])


def owned(features, query_pool, query_ids):
    ex_dev, modules, feat = features.shape
    peers = lax.axis_size("gx") * lax.axis_size("row")
    ids = jnp.concatenate([query_ids, exchange(query_ids, "pb", 1, 2)])[None, :]
    chunks = pack(features, peers)
    for k in ORDER[:-1]:
        chunks[k] = exchange(chunks[k], GROUP, k, peers)
    picked = pick(query_pool, ids)
    ahead = early([chunks[k] for k in AHEAD], feat)
    own, other = score([chunks[k] for k in LATE], ahead, picked, modules)
    part = own + exchange(other, "pb", 1, 2).astype(F32)
    near = part[0]
    for k in NEAR:
        near = near + exchange(part[k].astype(BF16), GROUP, k, peers).astype(F32)
    return near[0] + exchange(near[1].astype(BF16), GROUP, 4, peers).astype(F32)


def regrouped(features, query_pool, query_ids):
    ex_dev, modules, feat = features.shape
    regrouped = lax.all_to_all(features, "gx", split_axis=1, concat_axis=0, tiled=True)
    count = regrouped.shape[0] * lax.axis_size("row")
    grams = jnp.einsum("emk,emj->mkj", regrouped, regrouped, preferred_element_type=jnp.float32)
    grams = lax.psum(grams, "row")
    total = lax.psum(jnp.sum(jnp.trace(grams, axis1=1, axis2=2)), "gx")
    damping = 0.5 * total / (count * modules * feat)
    identity = jnp.eye(feat, dtype=jnp.float32)
    hessian = grams / count + damping * identity
    frob = jnp.sqrt(jnp.sum(hessian * hessian, axis=(1, 2)) + 1e-06)
    inverse = identity[None] / frob[:, None, None]
    for step in range(ITERS):
        product = jnp.matmul(hessian, inverse, precision=lax.Precision.HIGHEST)
        inverse = 2.0 * inverse - jnp.matmul(inverse, product, precision=lax.Precision.HIGHEST)
    picked = jnp.take(query_pool, query_ids, axis=0)
    precond = jnp.einsum(
        "qmk,mkj->qmj", picked.astype(jnp.float32), inverse, precision=lax.Precision.HIGHEST
    ).astype(jnp.bfloat16)
    local_queries = precond.shape[0]
    flat_query = precond.reshape(local_queries, -1)
    return lax.psum_scatter(
        jnp.einsum(
            "ea,qa->eq",
            regrouped.reshape(ex_dev * lax.axis_size("gx"), -1),
            flat_query,
            preferred_element_type=jnp.float32,
        ),
        "gx",
        scatter_dimension=0,
        tiled=True,
    )


def shards(features, query_pool, query_ids):
    modules = features.shape[1]
    gx, row, pb = (lax.axis_size(name) for name in ("gx", "row", "pb"))
    if (gx, row, pb) == (4, 2, 2) and modules == gx * row * pb:
        return owned(features, query_pool, query_ids)
    return regrouped(features, query_pool, query_ids)


def solution(mesh):
    in_specs = (P(("grp", "gx", "row"), None, None), P(None, "gx", None), P("pb"))
    out_specs = P(("grp", "gx", "row"), "pb")
    return jax.shard_map(shards, mesh=mesh, in_specs=in_specs, out_specs=out_specs, check_vma=False)
```
